512 devices in a mesh: energy: 32 (over x, z_lo), momentum: 16 (over z_hi, y, core).
Axes of the slice: x: 4, y: 4, z: 16 (z_hi: 2, z_lo: 8; z = z_hi * 8 + z_lo), core: 2. Of those that a mesh axis runs over, the one named last changes fastest.
Arguments:
- green_tiles: bfloat16 [16, 64, 4, 2, 128, 128], P('momentum', 'energy'), may hold values from -6 to 6
- dham_blocks: bfloat16 [3, 4, 2, 128, 128], replicated, may hold values from -0.375 to 0.375
- phonon_weight: float32 [6, 3, 2], replicated, may hold values from 0.1 to 0.5
- phonon_modes: int32 [6, 2], replicated, may hold values from -1 to 2, as said below
- tile_pattern: int32 [4, 2], replicated, may hold values from 0 to 3, as said below
Outputs:
- self_energy: bfloat16 [16, 64, 4, 2, 128, 128], P('momentum', 'energy')
The draws below stay inside these ranges and needn't reach their ends.
Inputs may be any that keep to these rules, and one draw needn't show every extreme that they name: `phonon_modes`: column 0 is a momentum offset and each of -1, 0, 1 is used by some mode; column 1 is an energy offset and each of 1 to 2 is used by some mode. `tile_pattern`: every block number appears in each column.
All inputs are finite; a program needn't handle non-finite values.
Results may differ from the reference program's by a relative error of at most 0.0062.
Values may be sent and summed in bfloat16 or wider, within the bound.
A program may use at most 64 MiB of HBM per device.

```python
import math
import jax
import jax.numpy as jnp
from jax import lax

TS = 128
NT = 4
NB = 4
NQ = 6
E_DEV = 2
NE = 64
NK = 16


def draw_phonon_modes(key, part):
    first = jax.random.fold_in(key, 11)
    second = jax.random.fold_in(key, 23)
    momentum_steps = jax.random.permutation(first, jnp.arange(NQ, dtype=jnp.int32) % 3) - 1
    energy_steps = jax.random.permutation(second, jnp.arange(NQ, dtype=jnp.int32) % E_DEV) + 1
    return jnp.stack([momentum_steps, energy_steps], axis=1).astype(jnp.int32)


def draw_tile_pattern(key, part):
    first = jax.random.fold_in(key, 37)
    second = jax.random.fold_in(key, 41)
    left_side = jax.random.permutation(first, jnp.arange(NT, dtype=jnp.int32) % NB)
    right_side = jax.random.permutation(second, jnp.arange(NT, dtype=jnp.int32) % NB)
    return jnp.stack([left_side, right_side], axis=1).astype(jnp.int32)


def block_scale(own_key, shape, pieces, low, largest):
    loudness, own = 1.0, jax.random.fold_in(own_key, 6)
    for axis_at, blocks in pieces:
        steps = jnp.exp(jax.random.uniform(jax.random.fold_in(own, axis_at), (blocks,), jnp.float32, low / len(pieces), largest / len(pieces)))
        loudness = loudness * jnp.repeat(steps, shape[axis_at] // blocks).reshape([-1 if axis == axis_at else 1 for axis in range(len(shape))])
    return loudness


def centred(rng, dims, spread, reach, pieces=(), held_as=jnp.bfloat16):
    result = spread * jax.random.normal(rng, dims, jnp.float32)
    if pieces:
        result = result * block_scale(rng, dims, pieces, -0.22, 0.18)
    return jnp.clip(result, -reach, reach).astype(held_as)


def setup_inputs(seed: int = 0) -> dict:
    splits = jax.random.split(jax.random.key(seed), 6)
    green_tiles = centred(splits[0], (NK, NE, NT, 2, TS, TS), 1.0, 6.0, ((0, 16), (1, 32)))
    dham_blocks = centred(splits[1], (3, NB, 2, TS, TS), (2 * TS) ** -0.5, 0.375)
    phonon_weight = jnp.clip(jnp.exp(jax.random.uniform(splits[2], (NQ, 3, 2), jnp.float32, math.log(0.1), math.log(0.5))), 0.1, 0.5)
    phonon_modes = draw_phonon_modes(jax.random.fold_in(splits[5], 71), 0)
    tile_pattern = draw_tile_pattern(jax.random.fold_in(splits[5], 71), 0)
    return {"green_tiles": green_tiles, "dham_blocks": dham_blocks, "phonon_weight": phonon_weight, "phonon_modes": phonon_modes, "tile_pattern": tile_pattern}


OFFSETS = (-1, 0, 1)


def stack_blocks(left_sel, right_sel):
    left_real = left_sel[:, :, 0]
    left_imag = left_sel[:, :, 1]
    upper_row = jnp.stack([left_real, -left_imag], axis=3)
    lower_row = jnp.stack([left_imag, left_real], axis=3)
    left_big = jnp.stack([upper_row, lower_row], axis=2)
    right_real = jnp.swapaxes(right_sel[:, :, 0], -1, -2)
    right_imag = jnp.swapaxes(right_sel[:, :, 1], -1, -2)
    first_col = jnp.stack([right_real, -right_imag], axis=3)
    second_col = jnp.stack([right_imag, right_real], axis=3)
    right_big = jnp.stack([first_col, second_col], axis=2)
    return left_big, right_big


def coupling(phonon_modes, phonon_weight, offset):
    span = jnp.arange(-E_DEV, E_DEV + 1, dtype=jnp.int32)
    chosen = (phonon_modes[:, 0] == offset).astype(jnp.float32)
    below = (span[None, :] == -phonon_modes[:, 1:2]).astype(jnp.float32)
    above = (span[None, :] == phonon_modes[:, 1:2]).astype(jnp.float32)
    terms = chosen[:, None, None] * (phonon_weight[:, :, 0:1] * below[:, None, :] + phonon_weight[:, :, 1:2] * above[:, None, :])
    return jnp.sum(terms, axis=0).astype(jnp.bfloat16)


def reference(green_tiles, dham_blocks, phonon_weight, phonon_modes, tile_pattern):
    left_big, right_big = stack_blocks(dham_blocks[:, tile_pattern[:, 0]], dham_blocks[:, tile_pattern[:, 1]])
    left_wide = left_big.astype(jnp.float32)
    right_wide = right_big.astype(jnp.float32)
    kernels = [coupling(phonon_modes, phonon_weight, offset).astype(jnp.float32) for offset in OFFSETS]

    def one_momentum(momentum):
        summed = jnp.zeros((NE, NT, 2, TS, TS), jnp.float32)
        for position, offset in enumerate(OFFSETS):
            source = ((momentum - offset) % NK).astype(jnp.int32)
            tiles = lax.dynamic_index_in_dim(green_tiles, source, 0, keepdims=False)
            padded = jnp.pad(tiles, ((E_DEV, E_DEV), (0, 0), (0, 0), (0, 0), (0, 0)))
            kern = kernels[position]
            accum = jnp.zeros((3, NE, NT, 2, TS, TS), jnp.float32)
            for column in range(2 * E_DEV + 1):
                segment = padded[column:column + NE].astype(jnp.float32)
                accum = accum + kern[:, column][:, None, None, None, None, None] * segment[None]
            mixed = accum.astype(jnp.bfloat16).astype(jnp.float32)
            product = jnp.einsum("dtbicj,detcjk->detbik", left_wide, mixed).astype(jnp.bfloat16)
            summed = summed + jnp.einsum("detcij,dtcjbk->etbik", product.astype(jnp.float32), right_wide)
        return summed.astype(jnp.bfloat16)

    return lax.map(one_momentum, jnp.arange(NK, dtype=jnp.int32))
```

```python
import jax
import jax.numpy as jnp
from jax import lax
from jax.sharding import PartitionSpec as P

OFFSETS = (-1, 0, 1)


def with_halo(block, sides, width):
    for axis, dim in sides:
        count = lax.axis_size(axis)
        forward = [(i, i + 1) for i in range(count - 1)]
        backward = [(target, source) for source, target in forward]
        low = lax.ppermute(
            lax.slice_in_dim(block, block.shape[dim] - width, None, axis=dim), axis, forward
        )
        high = lax.ppermute(lax.slice_in_dim(block, 0, width, axis=dim), axis, backward)
        block = jnp.concatenate([low, block, high], axis=dim)
    return block


def from_behind(block, axis, distance):
    devices = range(lax.axis_size(axis))
    route = [((i - distance) % len(devices), i) for i in devices]
    return lax.ppermute(block, axis, route)


def stack_blocks(left_sel, right_sel):
    left_real = left_sel[:, :, 0]
    left_imag = left_sel[:, :, 1]
    upper_row = jnp.stack([left_real, -left_imag], axis=3)
    lower_row = jnp.stack([left_imag, left_real], axis=3)
    left_big = jnp.stack([upper_row, lower_row], axis=2)
    right_real = jnp.swapaxes(right_sel[:, :, 0], -1, -2)
    right_imag = jnp.swapaxes(right_sel[:, :, 1], -1, -2)
    first_col = jnp.stack([right_real, -right_imag], axis=3)
    second_col = jnp.stack([right_imag, right_real], axis=3)
    right_big = jnp.stack([first_col, second_col], axis=2)
    return (left_big, right_big)


def coupling(phonon_modes, phonon_weight, offset, energy_count):
    span = jnp.arange(-energy_count, energy_count + 1, dtype=jnp.int32)
    chosen = (phonon_modes[:, 0] == offset).astype(jnp.float32)
    below = (span[None, :] == -phonon_modes[:, 1:2]).astype(jnp.float32)
    above = (span[None, :] == phonon_modes[:, 1:2]).astype(jnp.float32)
    terms = chosen[:, None, None] * (
        phonon_weight[:, :, 0:1] * below[:, None, :] + phonon_weight[:, :, 1:2] * above[:, None, :]
    )
    return jnp.sum(terms, axis=0).astype(jnp.bfloat16)


def band_matrix(kern, energy_count):
    relative = (
        jnp.arange(3 * energy_count, dtype=jnp.int32)[None, :]
        - energy_count
        - jnp.arange(energy_count, dtype=jnp.int32)[:, None]
    )
    span = jnp.arange(-energy_count, energy_count + 1, dtype=jnp.int32)
    onehot = (relative[:, :, None] == span[None, None, :]).astype(jnp.float32)
    table = jnp.einsum(
        "dx,ejx->dej", kern.astype(jnp.float32), onehot, precision=lax.Precision.HIGHEST
    )
    return table.astype(jnp.bfloat16).reshape(3 * energy_count, 3 * energy_count)


def contribution(window, table, left_big, right_big):
    energy_count = window.shape[0] // 3
    flat = window.reshape(window.shape[0], -1)
    mixed = jnp.dot(table, flat, preferred_element_type=jnp.float32).astype(jnp.bfloat16)
    mixed = mixed.reshape((3, energy_count) + window.shape[1:])
    product = jnp.einsum(
        "dtbicj,detcjk->detbik", left_big, mixed, preferred_element_type=jnp.float32
    ).astype(jnp.bfloat16)
    return jnp.einsum(
        "detcij,dtcjbk->etbik", product, right_big, preferred_element_type=jnp.float32
    )


def local(green_tiles, dham_blocks, phonon_weight, phonon_modes, tile_pattern):
    energy_count = green_tiles.shape[1]
    tile_count = green_tiles.shape[2]
    tile_size = green_tiles.shape[4]
    block_count = dham_blocks.shape[1]
    block_ids = jnp.arange(block_count, dtype=jnp.int32)[None, :]
    choose_left = (tile_pattern[:, 0:1] == block_ids).astype(jnp.bfloat16)
    choose_right = (tile_pattern[:, 1:2] == block_ids).astype(jnp.bfloat16)
    left_sel = jnp.einsum(
        "tb,dbcij->dtcij", choose_left, dham_blocks, preferred_element_type=jnp.float32
    ).astype(jnp.bfloat16)
    right_sel = jnp.einsum(
        "tb,dbcij->dtcij", choose_right, dham_blocks, preferred_element_type=jnp.float32
    ).astype(jnp.bfloat16)
    left_big, right_big = stack_blocks(left_sel, right_sel)
    tables = [
        band_matrix(coupling(phonon_modes, phonon_weight, offset, energy_count), energy_count)
        for offset in OFFSETS
    ]
    packed = green_tiles.reshape(1, energy_count * tile_count, 2, tile_size, tile_size)
    window_shape = (3 * energy_count, tile_count, 2, tile_size, tile_size)
    summed = jnp.zeros((energy_count, tile_count, 2, tile_size, tile_size), jnp.float32)
    own_window = with_halo(packed, (("energy", 0),), 1)
    for position, offset in enumerate(OFFSETS):
        term = contribution(own_window.reshape(window_shape), tables[position], left_big, right_big)
        if offset != 0:
            term = from_behind(term.astype(jnp.bfloat16), "momentum", offset).astype(jnp.float32)
        summed = summed + term
    return summed.astype(jnp.bfloat16)[None]


def solution(mesh):
    placed = (P("momentum", "energy", None, None, None, None), P(), P(), P(), P())
    return jax.shard_map(
        local,
        mesh=mesh,
        in_specs=placed,
        out_specs=P("momentum", "energy", None, None, None, None),
        check_vma=False,
    )
```

```python
import functools

import jax
import jax.numpy as jnp
from jax import lax
from jax.experimental import pallas as pl
from jax.experimental.pallas import tpu as pltpu
from jax.sharding import PartitionSpec as P

MESH = pl.DeviceIdType.MESH
F32, BF16 = jnp.float32, jnp.bfloat16
ZLO, YS, CORES, EB, NB, RANGE = 8, 4, 2, 2, 3, 2
SPAN = 2 * RANGE + 1
ROWS = 16


def spot(e, k):
    return {"energy": e, "momentum": k}


def kernel(
    ne, nk, weight, modes, pattern, green, dham, out,
    mine, blocks, coef, left, right, mixed, prod, near, passing, part, gained, own,
    load_sem, m_send, m_recv, r_send, r_recv, e_send, e_recv,
):
    nt, ts = green.shape[1], green.shape[3]
    e, k = lax.axis_index("energy"), lax.axis_index("momentum")
    core, y, z_hi = k % CORES, (k // CORES) % YS, k // (CORES * YS)
    z_lo, x = e % ZLO, e // ZLO

    def at(plane, c, side):
        turn = jnp.where(z_lo < ZLO // 2, side, 1 - side)
        return spot(
            x * ZLO + (z_lo + ZLO // 2) % ZLO, (((z_hi + turn) % 2) * YS + plane) * CORES + c
        )

    up_far = jnp.logical_and(y == YS - 1, core == 1)
    down_far = jnp.logical_and(y == 0, core == 0)
    relays = jnp.logical_or(y == 1, y == 2)
    above, below = (k + 1) % nk, (k + nk - 1) % nk

    loads = [
        pltpu.make_async_copy(green, mine, load_sem.at[0]),
        pltpu.make_async_copy(dham, blocks, load_sem.at[1]),
    ]
    for load in loads:
        load.start()

    barrier = pltpu.get_barrier_semaphore()

    def greet(where):
        pl.semaphore_signal(barrier, inc=1, device_id=where, device_id_type=MESH)

    @pl.when(down_far)
    def _():
        greet(at(2, 0, 1))
        greet(at(2, 1, 0))

    @pl.when(jnp.logical_not(down_far))
    def _():
        greet(spot(e, below))

    @pl.when(up_far)
    def _():
        greet(at(1, 0, 1))
        greet(at(1, 1, 0))

    @pl.when(jnp.logical_not(up_far))
    def _():
        greet(spot(e, above))

    def relay_source():
        return (y == 2), (core == 0)

    for plane, (source_y, source_c) in ((1, (0, 0)), (2, (YS - 1, 1))):
        for c in (0, 1):

            @pl.when(jnp.logical_and(y == plane, core == c))
            def _():
                greet(at(source_y, source_c, 1 - c))

    @pl.when(e > 0)
    def _():
        greet(spot(e - 1, k))

    @pl.when(e < ne - 1)
    def _():
        greet(spot(e + 1, k))

    lane = lax.broadcasted_iota(jnp.int32, (8, 128), 1)
    row = lax.broadcasted_iota(jnp.int32, (8, 128), 0)
    lane_q, lane_s = lane // SPAN - 1, lane % SPAN - RANGE
    table = jnp.zeros((8, 128), F32)
    for m in range(modes.shape[0]):
        emit, absorb = [
            jnp.where(row == 0, weight[m, 0, i], jnp.where(row == 1, weight[m, 1, i], weight[m, 2, i]))
            for i in (0, 1)
        ]
        step = modes[m, 1]
        term = jnp.where(lane_s == -step, emit, 0.0) + jnp.where(lane_s == step, absorb, 0.0)
        table = table + jnp.where(lane_q == modes[m, 0], term, 0.0)
    table = table.astype(BF16).astype(F32)
    for q in range(3):
        for d in range(3):
            for s in range(SPAN):
                at_lane = q * SPAN + s
                coef[(q * 3 + d) * SPAN + s] = jnp.broadcast_to(
                    table[d : d + 1, at_lane : at_lane + 1], (8, 128)
                )

    loads[1].wait()

    def stack(t, _):
        for d in range(3):
            re, im = blocks[d, pattern[t, 0], 0], blocks[d, pattern[t, 0], 1]
            left[t, d, :ts, :ts] = re
            left[t, d, :ts, ts:] = -im
            left[t, d, ts:, :ts] = im
            left[t, d, ts:, ts:] = re
            re = blocks[d, pattern[t, 1], 0].astype(F32).T.astype(BF16)
            im = blocks[d, pattern[t, 1], 1].astype(F32).T.astype(BF16)
            base = 2 * ts * d
            right[t, base : base + ts, :ts] = re
            right[t, base : base + ts, ts:] = -im
            right[t, base + ts : base + 2 * ts, :ts] = im
            right[t, base + ts : base + 2 * ts, ts:] = re
        return 0

    lax.fori_loop(0, nt, stack, 0)

    @pl.when(e == 0)
    def _():
        gained[0] = jnp.zeros(gained.shape[1:], BF16)

    @pl.when(e == ne - 1)
    def _():
        gained[1] = jnp.zeros(gained.shape[1:], BF16)

    far = jnp.logical_or(up_far, down_far)
    pl.semaphore_wait(
        barrier,
        2
        + far.astype(jnp.int32)
        + relays.astype(jnp.int32)
        + (e > 0).astype(jnp.int32)
        + (e < ne - 1).astype(jnp.int32),
    )

    def direct(t, i, way):
        target = above if way == 0 else below
        return pltpu.make_async_remote_copy(
            src_ref=green.at[i, t], dst_ref=near.at[way, t, i],
            send_sem=m_send.at[way, t, i], recv_sem=m_recv.at[way, t, i],
            device_id=spot(e, target), device_id_type=MESH,
        )

    def detour(t, i, way):
        return pltpu.make_async_remote_copy(
            src_ref=green.at[i, t], dst_ref=passing.at[t],
            send_sem=m_send.at[way, t, i], recv_sem=r_recv.at[t],
            device_id=at(2 if way == 0 else 1, i, i), device_id_type=MESH,
        )

    def forward(t, plane, c):
        goal_y, goal_c, way = (0, 0, 0) if plane == 2 else (YS - 1, 1, 1)
        return pltpu.make_async_remote_copy(
            src_ref=passing.at[t], dst_ref=near.at[way, t, c],
            send_sem=r_send.at[t], recv_sem=m_recv.at[way, t, c],
            device_id=at(goal_y, goal_c, c), device_id_type=MESH,
        )

    def send_raw(t, _):
        for way, is_far in ((0, up_far), (1, down_far)):
            for i in range(EB):

                @pl.when(is_far)
                def _():
                    detour(t, i, way).start()

                @pl.when(jnp.logical_not(is_far))
                def _():
                    direct(t, i, way).start()

        return 0

    lax.fori_loop(0, nt, send_raw, 0)
    loads[0].wait()

    outer = [0, 1, 4, 5]
    inner = [2, 3]

    def contract(t, targets):
        width = len(targets) * ts

        def mix(c):
            def rows(j, _):
                at_row = pl.multiple_of(j * ROWS, ROWS)
                tiles = [
                    [
                        ref[c, pl.ds(at_row, ROWS), :].astype(F32).reshape(ROWS // 8, 8, ts)
                        for ref in refs
                    ]
                    for refs in (
                        [near.at[1, t, i] for i in range(EB)],
                        [mine.at[i, t] for i in range(EB)],
                        [near.at[0, t, i] for i in range(EB)],
                    )
                ]
                for d in range(3):
                    for n, target in enumerate(targets):
                        total = None
                        for i in range(EB):
                            s = i - (target - RANGE)
                            if abs(s) > RANGE:
                                continue
                            for q in range(3):
                                value = coef[(q * 3 + d) * SPAN + s + RANGE][None] * tiles[q][i]
                                total = value if total is None else total + value
                        mixed[d, pl.ds(c * ts + at_row, ROWS), n * ts : (n + 1) * ts] = (
                            total.reshape(ROWS, ts).astype(BF16)
                        )
                return 0

            lax.fori_loop(0, ts // ROWS, rows, 0)

        mix(0)
        mix(1)
        for d in range(3):
            got = jnp.dot(left[t, d], mixed[d, :, :width], preferred_element_type=F32).astype(BF16)
            for n in range(len(targets)):
                for c in range(2):
                    prod[n * ts : (n + 1) * ts, (2 * d + c) * ts : (2 * d + c + 1) * ts] = got[
                        c * ts : (c + 1) * ts, n * ts : (n + 1) * ts
                    ]
        return jnp.dot(prod[:width], right[t], preferred_element_type=F32)

    def shift(t, way):
        return pltpu.make_async_remote_copy(
            src_ref=part.at[way, t], dst_ref=gained.at[1 - way, t],
            send_sem=e_send.at[way, t], recv_sem=e_recv.at[1 - way, t],
            device_id=spot(e - 1 if way == 0 else e + 1, k), device_id_type=MESH,
        )

    def tile(t, _):
        for side in (0, 1):
            for i in range(EB):
                direct(t, i, side).wait_recv()
        total = contract(t, outer)
        for n in range(4):
            for c in range(2):
                part[n // 2, t, n % 2, c] = total[
                    n * ts : (n + 1) * ts, c * ts : (c + 1) * ts
                ].astype(BF16)

        @pl.when(e > 0)
        def _():
            shift(t, 0).start()

        @pl.when(e < ne - 1)
        def _():
            shift(t, 1).start()

        for plane in (1, 2):
            for c in (0, 1):

                @pl.when(jnp.logical_and(y == plane, core == c))
                def _():
                    hop = forward(t, plane, c)
                    detour(t, c, 0).wait_recv()
                    hop.start()

        total = contract(t, inner)
        for n in range(2):
            for c in range(2):
                own[t, n, c] = total[n * ts : (n + 1) * ts, c * ts : (c + 1) * ts]
        return 0

    lax.fori_loop(0, nt, tile, 0)

    def finish(t, _):
        @pl.when(e > 0)
        def _():
            shift(t, 1).wait_recv()

        @pl.when(e < ne - 1)
        def _():
            shift(t, 0).wait_recv()

        for n in range(EB):
            out[n, t] = (
                own[t, n] + gained[0, t, n].astype(F32) + gained[1, t, n].astype(F32)
            ).astype(BF16)
        return 0

    lax.fori_loop(0, nt, finish, 0)

    def drain(t, _):
        for way in (0, 1):
            for i in range(EB):
                direct(t, i, way).wait_send()

        @pl.when(e > 0)
        def _():
            shift(t, 0).wait_send()

        @pl.when(e < ne - 1)
        def _():
            shift(t, 1).wait_send()

        @pl.when(relays)
        def _():
            forward(t, 1, 0).wait_send()

        return 0

    lax.fori_loop(0, nt, drain, 0)


def solution(mesh):
    ne, nk = mesh.shape["energy"], mesh.shape["momentum"]

    def local(green_tiles, dham_blocks, phonon_weight, phonon_modes, tile_pattern):
        green = green_tiles[0]
        eb, nt, parts, ts, _ = green.shape
        dirs = dham_blocks.shape[0]
        sems = pltpu.SemaphoreType.DMA
        whole = pl.BlockSpec(memory_space=pltpu.SMEM)
        away = pl.BlockSpec(memory_space=pl.ANY)
        got = pl.pallas_call(
            functools.partial(kernel, ne, nk),
            out_shape=jax.ShapeDtypeStruct(green.shape, BF16),
            in_specs=[whole, whole, whole, away, away],
            out_specs=pl.BlockSpec(memory_space=pltpu.VMEM),
            scratch_shapes=[
                pltpu.VMEM(green.shape, BF16),
                pltpu.VMEM(dham_blocks.shape, BF16),
                pltpu.VMEM((3 * dirs * SPAN, 8, 128), F32),
                pltpu.VMEM((nt, dirs, 2 * ts, 2 * ts), BF16),
                pltpu.VMEM((nt, 2 * ts * dirs, 2 * ts), BF16),
                pltpu.VMEM((dirs, 2 * ts, 4 * ts), BF16),
                pltpu.VMEM((4 * ts, 2 * ts * dirs), BF16),
                pltpu.VMEM((2, nt, eb, parts, ts, ts), BF16),
                pltpu.VMEM((nt, parts, ts, ts), BF16),
                pltpu.VMEM((2, nt, eb, parts, ts, ts), BF16),
                pltpu.VMEM((2, nt, eb, parts, ts, ts), BF16),
                pltpu.VMEM((nt, eb, parts, ts, ts), F32),
                sems((2,)),
                sems((2, nt, eb)),
                sems((2, nt, eb)),
                sems((nt,)),
                sems((nt,)),
                sems((2, nt)),
                sems((2, nt)),
            ],
            compiler_params=pltpu.CompilerParams(collective_id=0, has_side_effects=True),
        )(phonon_weight, phonon_modes, tile_pattern, green, dham_blocks)
        return got[None]

    placed = (P("momentum", "energy", None, None, None, None), P(), P(), P(), P())
    return jax.shard_map(
        local,
        mesh=mesh,
        in_specs=placed,
        out_specs=P("momentum", "energy", None, None, None, None),
        check_vma=False,
    )
```

```python
import functools

import jax
import jax.numpy as jnp
from jax import lax
from jax.experimental import pallas as pl
from jax.experimental.pallas import tpu as pltpu
from jax.sharding import PartitionSpec as P

MESH = pl.DeviceIdType.MESH
F32, BF16 = jnp.float32, jnp.bfloat16
ND, H0, H1, HF0, HF1 = 1, 1, 0, 1, 1
ZLO, YS, CORES, EB, NB, RANGE = 8, 4, 2, 2, 3, 2
SPAN = 2 * RANGE + 1
ROWS = 16


def spot(e, k):
    return {"energy": e, "momentum": k}


def kernel(
    ne, nk, weight, modes, pattern, green, dham, own, from_below, from_above,
    mine, blocks, coef, left, right, mixed, prod, near, passing, part, ready,
    load_sem, m_send, m_recv, r_send, r_recv, e_send, e_recv,
):
    nt, ts = green.shape[1], green.shape[3]
    e, k = lax.axis_index("energy"), lax.axis_index("momentum")
    core, y, z_hi = k % CORES, (k // CORES) % YS, k // (CORES * YS)
    z_lo, x = e % ZLO, e // ZLO

    def at(plane, c, side):
        turn = jnp.where(z_lo < ZLO // 2, side, 1 - side)
        return spot(
            x * ZLO + (z_lo + ZLO // 2) % ZLO, (((z_hi + turn) % 2) * YS + plane) * CORES + c
        )

    up_far = jnp.logical_and(y == YS - 1, core == 1)
    down_far = jnp.logical_and(y == 0, core == 0)
    relays = jnp.logical_or(y == 1, y == 2)
    above, below = (k + 1) % nk, (k + nk - 1) % nk

    loads = [
        pltpu.make_async_copy(green, mine, load_sem.at[0]),
        pltpu.make_async_copy(dham, blocks, load_sem.at[1]),
    ]
    for load in loads:
        load.start()

    barrier = pltpu.get_barrier_semaphore()

    def greet(where):
        pl.semaphore_signal(barrier, inc=1, device_id=where, device_id_type=MESH)

    z = z_hi * ZLO + z_lo
    ahead, behind = (z + ZLO // 2) % (2 * ZLO), (z + 3 * ZLO // 2) % (2 * ZLO)

    def answered(source, target):
        return jnp.logical_and(source < ZLO, target > source)

    def relayed(source, target):
        return jnp.logical_or(target >= ZLO, answered(source, target))

    def also(flag, other):
        return jnp.logical_and(flag, other)

    def no(flag):
        return jnp.logical_not(flag)

    count, answers = jnp.int32(0), []

    def meet(flag, where):
        pl.when(flag)(lambda: greet(where))

    def expect(flag):
        nonlocal count
        count = count + flag.astype(jnp.int32)

    meet(no(down_far), spot(e, below))
    meet(no(up_far), spot(e, above))
    expect(no(down_far))
    expect(no(up_far))
    low_end, high_end = also(z_lo == 0, e > 0), also(z_lo == ZLO - 1, e < ne - 1)
    meet(e > 0, spot(e - 1, k))
    meet(also(e < ne - 1, no(also(high_end, z_hi == 0))), spot(e + 1, k))
    expect(also(e > 0, no(also(low_end, z_hi == 0))))
    expect(e < ne - 1)
    answers.append((also(high_end, z_hi == 0), spot(e + 1, k), 3))
    far_waits, relay_waits = [], jnp.bool_(False)
    for mine_far, out_plane, in_plane in ((up_far, 2, 1), (down_far, 1, 2)):
        for c, (there, back) in enumerate(((ahead, behind), (behind, ahead))):
            late = answered(z, there)
            meet(also(mine_far, late), at(out_plane, c, c))
            expect(also(mine_far, no(late)))
            if mine_far is up_far:
                far_waits.append(late)
            late = relayed(back, z)
            meet(also(mine_far, no(late)), at(in_plane, c, 1 - c))
            expect(also(mine_far, late))
            answers.append((also(mine_far, late), at(in_plane, c, 1 - c), 2))
    for mine_far, end in ((up_far, spot(e, above)), (down_far, spot(e, below))):
        if ND:
            meet(also(mine_far, z_hi == 0), end)
            expect(also(mine_far, z_hi == 1))
            answers.append((also(mine_far, z_hi == 1), end, 4))
    for plane, source, goal in ((1, (0, 0), (YS - 1, 1)), (2, (YS - 1, 1), (0, 0))):
        for c, (there, back) in enumerate(((ahead, behind), (behind, ahead))):
            here = also(y == plane, core == c)
            late = answered(back, z)
            meet(also(here, no(late)), at(*source, 1 - c))
            expect(also(here, late))
            answers.append((also(here, late), at(*source, 1 - c), c))
            late = relayed(z, there)
            meet(also(here, late), at(*goal, c))
            expect(also(here, no(late)))
            relay_waits = jnp.logical_or(relay_waits, also(here, late))

    pl.semaphore_wait(barrier, count)
    for flag, where, slot in answers:

        @pl.when(flag)
        def _():
            pl.semaphore_signal(ready.at[slot], inc=1, device_id=where, device_id_type=MESH)

    far = jnp.logical_or(up_far, down_far)

    def direct(t, i, way):
        target = above if way == 0 else below
        return pltpu.make_async_remote_copy(
            src_ref=green.at[i, t], dst_ref=near.at[way, t, i],
            send_sem=m_send.at[way, t, i], recv_sem=m_recv.at[way, t, i],
            device_id=spot(e, target), device_id_type=MESH,
        )

    def detour(t, i, way):
        return pltpu.make_async_remote_copy(
            src_ref=green.at[i, t], dst_ref=passing.at[t],
            send_sem=m_send.at[way, t, i], recv_sem=r_recv.at[t],
            device_id=at(2 if way == 0 else 1, i, i), device_id_type=MESH,
        )

    def forward(t, plane, c):
        goal_y, goal_c, way = (0, 0, 0) if plane == 2 else (YS - 1, 1, 1)
        return pltpu.make_async_remote_copy(
            src_ref=passing.at[t], dst_ref=near.at[way, t, c],
            send_sem=r_send.at[t], recv_sem=m_recv.at[way, t, c],
            device_id=at(goal_y, goal_c, c), device_id_type=MESH,
        )

    def send_near(t, _):
        for way, is_far in ((0, up_far), (1, down_far)):
            for i in range(EB):

                @pl.when(no(is_far))
                def _():
                    direct(t, i, way).start()

        return 0

    lax.fori_loop(0, nt, send_near, 0)
    for i in range(EB):

        @pl.when(also(far, far_waits[i]))
        def _():
            pl.semaphore_wait(ready.at[i], 1)

    for way, is_far in ((0, up_far), (1, down_far)):

        @pl.when(is_far)
        def _():
            def send_far(t, _):
                for i in range(EB):
                    detour(t, i, way).start()
                return 0

            def send_straight(t, _):
                for i in range(EB):
                    direct(t, i, way).start()
                return 0

            lax.fori_loop(0, nt - ND, send_far, 0)
            if ND:

                @pl.when(z_hi == 0)
                def _():
                    pl.semaphore_wait(ready.at[4], 1)

                lax.fori_loop(nt - ND, nt, send_straight, 0)

    blank = [
        pltpu.make_async_copy(part.at[0], from_below, load_sem.at[2]),
        pltpu.make_async_copy(part.at[0], from_above, load_sem.at[2]),
    ]
    for edge, copy in zip((e == 0, e == ne - 1), blank):

        @pl.when(edge)
        def _():
            part[0] = jnp.zeros(part.shape[1:], BF16)
            copy.start()
            copy.wait()

    lane = lax.broadcasted_iota(jnp.int32, (8, 128), 1)
    row = lax.broadcasted_iota(jnp.int32, (8, 128), 0)
    lane_q, lane_s = lane // SPAN - 1, lane % SPAN - RANGE
    table = jnp.zeros((8, 128), F32)
    for m in range(modes.shape[1]):
        emit, absorb = [
            jnp.where(row == 0, weight[0, i, m], jnp.where(row == 1, weight[1, i, m], weight[2, i, m]))
            for i in (0, 1)
        ]
        step = modes[1, m]
        term = jnp.where(lane_s == -step, emit, 0.0) + jnp.where(lane_s == step, absorb, 0.0)
        table = table + jnp.where(lane_q == modes[0, m], term, 0.0)
    table = table.astype(BF16).astype(F32)
    for q in range(3):
        for d in range(3):
            for s in range(SPAN):
                at_lane = q * SPAN + s
                coef[(q * 3 + d) * SPAN + s] = jnp.broadcast_to(
                    table[d : d + 1, at_lane : at_lane + 1], (8, 128)
                )

    loads[1].wait()

    def stack(t, _):
        for d in range(3):
            re, im = blocks[d, pattern[0, t], 0], blocks[d, pattern[0, t], 1]
            left[t, d, :ts, :ts] = re
            left[t, d, :ts, ts:] = -im
            left[t, d, ts:, :ts] = im
            left[t, d, ts:, ts:] = re
            re = blocks[d, pattern[1, t], 0].astype(F32).T.astype(BF16)
            im = blocks[d, pattern[1, t], 1].astype(F32).T.astype(BF16)
            base = 2 * ts * d
            right[t, base : base + ts, :ts] = re
            right[t, base : base + ts, ts:] = -im
            right[t, base + ts : base + 2 * ts, :ts] = im
            right[t, base + ts : base + 2 * ts, ts:] = re
        return 0

    lax.fori_loop(0, nt, stack, 0)

    loads[0].wait()

    outer = [0, 1, 4, 5]
    inner = [2, 3]

    def contract(t, targets):
        width = len(targets) * ts

        def mix(c):
            def rows(j, _):
                at_row = pl.multiple_of(j * ROWS, ROWS)
                tiles = [
                    [
                        ref[c, pl.ds(at_row, ROWS), :].astype(F32).reshape(ROWS // 8, 8, ts)
                        for ref in refs
                    ]
                    for refs in (
                        [near.at[1, t, i] for i in range(EB)],
                        [mine.at[i, t] for i in range(EB)],
                        [near.at[0, t, i] for i in range(EB)],
                    )
                ]
                for d in range(3):
                    for n, target in enumerate(targets):
                        total = None
                        for i in range(EB):
                            s = i - (target - RANGE)
                            if abs(s) > RANGE:
                                continue
                            for q in range(3):
                                value = coef[(q * 3 + d) * SPAN + s + RANGE][None] * tiles[q][i]
                                total = value if total is None else total + value
                        mixed[d, pl.ds(c * ts + at_row, ROWS), n * ts : (n + 1) * ts] = (
                            total.reshape(ROWS, ts).astype(BF16)
                        )
                return 0

            lax.fori_loop(0, ts // ROWS, rows, 0)

        mix(0)
        mix(1)
        for d in range(3):
            got = jnp.dot(left[t, d], mixed[d, :, :width], preferred_element_type=F32).astype(BF16)
            for n in range(len(targets)):
                for c in range(2):
                    prod[n * ts : (n + 1) * ts, (2 * d + c) * ts : (2 * d + c + 1) * ts] = got[
                        c * ts : (c + 1) * ts, n * ts : (n + 1) * ts
                    ]
        return jnp.dot(prod[:width], right[t], preferred_element_type=F32)

    def shift(t, way):
        return pltpu.make_async_remote_copy(
            src_ref=part.at[way, :, t], dst_ref=(from_above if way == 0 else from_below).at[:, t],
            send_sem=e_send.at[way, t], recv_sem=e_recv.at[1 - way, t],
            device_id=spot(e - 1 if way == 0 else e + 1, k), device_id_type=MESH,
        )

    early = z_hi == 0
    slow = also(low_end, early)

    def hold_near(t):
        return also(relays, t >= jnp.where(early, H0, H1))

    def hold_far(t):
        return also(relays, t >= jnp.where(early, HF0, HF1))

    ways = ((0, e > 0, z_lo == 0), (1, e < ne - 1, z_lo == ZLO - 1))

    def send_parts(t, long, flag):
        for way, there, is_long in ways:

            @pl.when(also(also(there, flag), is_long if long else no(is_long)))
            def _():
                shift(t, way).start()

    def relay(t, _):
        for plane in (1, 2):
            for c in (0, 1):

                @pl.when(also(y == plane, core == c))
                def _():
                    hop = forward(t, plane, c)
                    detour(t, c, 0).wait_recv()

                    @pl.when(also(relay_waits, t == 0))
                    def _():
                        pl.semaphore_wait(ready.at[2], 1)

                    hop.start()

        return 0

    def tile(t, _):
        for side in (0, 1):
            for i in range(EB):
                direct(t, i, side).wait_recv()
        total = contract(t, outer)
        for n in range(4):
            for c in range(2):
                part[n // 2, n % 2, t, c] = total[
                    n * ts : (n + 1) * ts, c * ts : (c + 1) * ts
                ].astype(BF16)

        send_parts(t, True, no(jnp.logical_or(slow, hold_far(t))))
        send_parts(t, False, no(hold_near(t)))

        @pl.when(also(also(relays, no(early)), t < nt - ND))
        def _():
            relay(t, 0)

        total = contract(t, inner)
        for n in range(2):
            for c in range(2):
                own[n, t, c] = total[n * ts : (n + 1) * ts, c * ts : (c + 1) * ts]
        return 0

    lax.fori_loop(0, nt, tile, 0)

    def slow_parts(t, _):
        send_parts(t, True, slow)
        return 0

    @pl.when(slow)
    def _():
        pl.semaphore_wait(ready.at[3], 1)
        lax.fori_loop(0, nt, slow_parts, 0)

    @pl.when(also(relays, early))
    def _():
        lax.fori_loop(0, nt - ND, relay, 0)

    def late(t, _):
        send_parts(t, True, also(hold_far(t), no(slow)))
        send_parts(t, False, hold_near(t))
        return 0

    @pl.when(relays)
    def _():
        lax.fori_loop(0, nt, late, 0)

    def finish(t, _):
        @pl.when(e > 0)
        def _():
            shift(t, 1).wait_recv()

        @pl.when(e < ne - 1)
        def _():
            shift(t, 0).wait_recv()

        return 0

    lax.fori_loop(0, nt, finish, 0)

    def drain(t, _):
        for way in (0, 1):
            for i in range(EB):
                direct(t, i, way).wait_send()

        @pl.when(e > 0)
        def _():
            shift(t, 0).wait_send()

        @pl.when(e < ne - 1)
        def _():
            shift(t, 1).wait_send()

        @pl.when(also(relays, t < nt - ND))
        def _():
            forward(t, 1, 0).wait_send()

        return 0

    lax.fori_loop(0, nt, drain, 0)


def solution(mesh):
    ne, nk = mesh.shape["energy"], mesh.shape["momentum"]

    def local(green_tiles, dham_blocks, phonon_weight, phonon_modes, tile_pattern):
        green = green_tiles[0]
        eb, nt, parts, ts, _ = green.shape
        dirs = dham_blocks.shape[0]
        sems = pltpu.SemaphoreType.DMA
        whole = pl.BlockSpec(memory_space=pltpu.SMEM)
        away = pl.BlockSpec(memory_space=pl.ANY)
        own, from_below, from_above = pl.pallas_call(
            functools.partial(kernel, ne, nk),
            out_shape=[jax.ShapeDtypeStruct(green.shape, kind) for kind in (F32, BF16, BF16)],
            in_specs=[whole, whole, whole, away, away],
            out_specs=[pl.BlockSpec(memory_space=pltpu.VMEM), away, away],
            scratch_shapes=[
                pltpu.VMEM(green.shape, BF16),
                pltpu.VMEM(dham_blocks.shape, BF16),
                pltpu.VMEM((3 * dirs * SPAN, 8, 128), F32),
                pltpu.VMEM((nt, dirs, 2 * ts, 2 * ts), BF16),
                pltpu.VMEM((nt, 2 * ts * dirs, 2 * ts), BF16),
                pltpu.VMEM((dirs, 2 * ts, 4 * ts), BF16),
                pltpu.VMEM((4 * ts, 2 * ts * dirs), BF16),
                pltpu.VMEM((2, nt, eb, parts, ts, ts), BF16),
                pltpu.VMEM((nt, parts, ts, ts), BF16),
                pltpu.VMEM((2, eb, nt, parts, ts, ts), BF16),
                pltpu.SemaphoreType.REGULAR((5,)),
                sems((3,)),
                sems((2, nt, eb)),
                sems((2, nt, eb)),
                sems((nt,)),
                sems((nt,)),
                sems((2, nt)),
                sems((2, nt)),
            ],
            compiler_params=pltpu.CompilerParams(collective_id=0, has_side_effects=True),
        )(phonon_weight.transpose(1, 2, 0), phonon_modes.T, tile_pattern.T, green, dham_blocks)
        return (own + from_below.astype(F32) + from_above.astype(F32)).astype(BF16)[None]

    placed = (P("momentum", "energy", None, None, None, None), P(), P(), P(), P())
    return jax.shard_map(
        local,
        mesh=mesh,
        in_specs=placed,
        out_specs=P("momentum", "energy", None, None, None, None),
        check_vma=False,
    )
```

```python
import functools

import jax
import jax.numpy as jnp
from jax import lax
from jax.experimental import pallas as pl
from jax.experimental.pallas import tpu as pltpu
from jax.sharding import PartitionSpec as P

MESH = pl.DeviceIdType.MESH
F32, BF16 = jnp.float32, jnp.bfloat16
ND, H0, H1, HF0, HF1 = 1, 1, 0, 1, 1
ZLO, YS, CORES, EB, NB, RANGE = 8, 4, 2, 2, 3, 2
SPAN = 2 * RANGE + 1
ROWS = 16


def spot(e, k):
    return {"energy": e, "momentum": k}


def kernel(
    ne, nk, weight, modes, pattern, green, dham, own_out, from_below, from_above,
    mine, blocks, coef, left, right, mixed, prod, near, passing, part, own, ready,
    load_sem, own_sem, m_send, m_recv, r_send, r_recv, e_send, e_recv,
):
    nt, ts = green.shape[1], green.shape[3]
    e, k = lax.axis_index("energy"), lax.axis_index("momentum")
    core, y, z_hi = k % CORES, (k // CORES) % YS, k // (CORES * YS)
    z_lo, x = e % ZLO, e // ZLO

    def at(plane, c, side):
        turn = jnp.where(z_lo < ZLO // 2, side, 1 - side)
        return spot(
            x * ZLO + (z_lo + ZLO // 2) % ZLO, (((z_hi + turn) % 2) * YS + plane) * CORES + c
        )

    up_far = jnp.logical_and(y == YS - 1, core == 1)
    down_far = jnp.logical_and(y == 0, core == 0)
    relays = jnp.logical_or(y == 1, y == 2)
    above, below = (k + 1) % nk, (k + nk - 1) % nk

    loads = [
        pltpu.make_async_copy(green, mine, load_sem.at[0]),
        pltpu.make_async_copy(dham, blocks, load_sem.at[1]),
    ]
    for load in loads:
        load.start()

    barrier = pltpu.get_barrier_semaphore()

    def greet(where):
        pl.semaphore_signal(barrier, inc=1, device_id=where, device_id_type=MESH)

    z = z_hi * ZLO + z_lo
    ahead, behind = (z + ZLO // 2) % (2 * ZLO), (z + 3 * ZLO // 2) % (2 * ZLO)

    def answered(source, target):
        return jnp.logical_and(source < ZLO, target > source)

    def relayed(source, target):
        return jnp.logical_or(target >= ZLO, answered(source, target))

    def also(flag, other):
        return jnp.logical_and(flag, other)

    def no(flag):
        return jnp.logical_not(flag)

    count, answers = jnp.int32(0), []

    def meet(flag, where):
        pl.when(flag)(lambda: greet(where))

    def expect(flag):
        nonlocal count
        count = count + flag.astype(jnp.int32)

    far_waits, relay_waits = [], jnp.bool_(False)
    for mine_far, out_plane, in_plane in ((up_far, 2, 1), (down_far, 1, 2)):
        for c, (there, back) in enumerate(((ahead, behind), (behind, ahead))):
            late = answered(z, there)
            meet(also(mine_far, late), at(out_plane, c, c))
            expect(also(mine_far, no(late)))
            if mine_far is up_far:
                far_waits.append(late)
            late = relayed(back, z)
            meet(also(mine_far, no(late)), at(in_plane, c, 1 - c))
            expect(also(mine_far, late))
            answers.append((also(mine_far, late), at(in_plane, c, 1 - c), 2))
    for mine_far, end in ((up_far, spot(e, above)), (down_far, spot(e, below))):
        if ND:
            meet(also(mine_far, z_hi == 0), end)
            expect(also(mine_far, z_hi == 1))
            answers.append((also(mine_far, z_hi == 1), end, 4))
    for plane, source, goal in ((1, (0, 0), (YS - 1, 1)), (2, (YS - 1, 1), (0, 0))):
        for c, (there, back) in enumerate(((ahead, behind), (behind, ahead))):
            here = also(y == plane, core == c)
            late = answered(back, z)
            meet(also(here, no(late)), at(*source, 1 - c))
            expect(also(here, late))
            answers.append((also(here, late), at(*source, 1 - c), c))
            late = relayed(z, there)
            meet(also(here, late), at(*goal, c))
            expect(also(here, no(late)))
            relay_waits = jnp.logical_or(relay_waits, also(here, late))

    meet(no(down_far), spot(e, below))
    meet(no(up_far), spot(e, above))
    expect(no(down_far))
    expect(no(up_far))
    low_end, high_end = also(z_lo == 0, e > 0), also(z_lo == ZLO - 1, e < ne - 1)
    meet(e > 0, spot(e - 1, k))
    meet(also(e < ne - 1, no(also(high_end, z_hi == 0))), spot(e + 1, k))
    expect(also(e > 0, no(also(low_end, z_hi == 0))))
    expect(e < ne - 1)
    answers.append((also(high_end, z_hi == 0), spot(e + 1, k), 3))
    pl.semaphore_wait(barrier, count)
    for flag, where, slot in answers:

        @pl.when(flag)
        def _():
            pl.semaphore_signal(ready.at[slot], inc=1, device_id=where, device_id_type=MESH)

    far = jnp.logical_or(up_far, down_far)

    def direct(t, i, way):
        target = above if way == 0 else below
        return pltpu.make_async_remote_copy(
            src_ref=green.at[i, t], dst_ref=near.at[way, t, i],
            send_sem=m_send.at[way, t, i], recv_sem=m_recv.at[way, t, i],
            device_id=spot(e, target), device_id_type=MESH,
        )

    def detour(t, i, way):
        return pltpu.make_async_remote_copy(
            src_ref=green.at[i, t], dst_ref=passing.at[t],
            send_sem=m_send.at[way, t, i], recv_sem=r_recv.at[t],
            device_id=at(2 if way == 0 else 1, i, i), device_id_type=MESH,
        )

    def forward(t, plane, c):
        goal_y, goal_c, way = (0, 0, 0) if plane == 2 else (YS - 1, 1, 1)
        return pltpu.make_async_remote_copy(
            src_ref=passing.at[t], dst_ref=near.at[way, t, c],
            send_sem=r_send.at[t], recv_sem=m_recv.at[way, t, c],
            device_id=at(goal_y, goal_c, c), device_id_type=MESH,
        )

    def send_near(t, _):
        for way, is_far in ((0, up_far), (1, down_far)):
            for i in range(EB):

                @pl.when(no(is_far))
                def _():
                    direct(t, i, way).start()

        return 0

    lax.fori_loop(0, nt, send_near, 0)
    for i in range(EB):

        @pl.when(also(far, far_waits[i]))
        def _():
            pl.semaphore_wait(ready.at[i], 1)

    for way, is_far in ((0, up_far), (1, down_far)):

        @pl.when(is_far)
        def _():
            def send_far(t, _):
                for i in range(EB):
                    detour(t, i, way).start()
                return 0

            def send_straight(t, _):
                for i in range(EB):
                    direct(t, i, way).start()
                return 0

            lax.fori_loop(0, nt - ND, send_far, 0)
            if ND:

                @pl.when(z_hi == 0)
                def _():
                    pl.semaphore_wait(ready.at[4], 1)

                lax.fori_loop(nt - ND, nt, send_straight, 0)

    blank = [
        pltpu.make_async_copy(part.at[0], from_below, load_sem.at[2]),
        pltpu.make_async_copy(part.at[0], from_above, load_sem.at[2]),
    ]
    for edge, copy in zip((e == 0, e == ne - 1), blank):

        @pl.when(edge)
        def _():
            part[0] = jnp.zeros(part.shape[1:], BF16)
            copy.start()
            copy.wait()

    lane = lax.broadcasted_iota(jnp.int32, (8, 128), 1)
    row = lax.broadcasted_iota(jnp.int32, (8, 128), 0)
    lane_q, lane_s = lane // SPAN - 1, lane % SPAN - RANGE
    table = jnp.zeros((8, 128), F32)
    for m in range(modes.shape[1]):
        emit, absorb = [
            jnp.where(row == 0, weight[0, i, m], jnp.where(row == 1, weight[1, i, m], weight[2, i, m]))
            for i in (0, 1)
        ]
        step = modes[1, m]
        term = jnp.where(lane_s == -step, emit, 0.0) + jnp.where(lane_s == step, absorb, 0.0)
        table = table + jnp.where(lane_q == modes[0, m], term, 0.0)
    table = table.astype(BF16).astype(F32)
    for q in range(3):
        for d in range(3):
            for s in range(SPAN):
                at_lane = q * SPAN + s
                coef[(q * 3 + d) * SPAN + s] = jnp.broadcast_to(
                    table[d : d + 1, at_lane : at_lane + 1], (8, 128)
                )

    loads[1].wait()

    def stack(t, _):
        for d in range(3):
            re, im = blocks[d, pattern[0, t], 0], blocks[d, pattern[0, t], 1]
            left[t, d, :ts, :ts] = re
            left[t, d, :ts, ts:] = -im
            left[t, d, ts:, :ts] = im
            left[t, d, ts:, ts:] = re
            re = blocks[d, pattern[1, t], 0].astype(F32).T.astype(BF16)
            im = blocks[d, pattern[1, t], 1].astype(F32).T.astype(BF16)
            base = 2 * ts * d
            right[t, base : base + ts, :ts] = re
            right[t, base : base + ts, ts:] = -im
            right[t, base + ts : base + 2 * ts, :ts] = im
            right[t, base + ts : base + 2 * ts, ts:] = re
        return 0

    lax.fori_loop(0, nt, stack, 0)

    loads[0].wait()

    outer = [[0, 1], [4, 5]]
    inner = [2, 3]

    def mix(t, targets, slot):
        sources = (
            [near.at[1, t, i] for i in range(EB)],
            [mine.at[i, t] for i in range(EB)],
            [near.at[0, t, i] for i in range(EB)],
        )
        for c in range(2):
            for j in range(0, ts, ROWS):
                tiles = [
                    [ref[c, j : j + ROWS, :].astype(F32).reshape(ROWS // 8, 8, ts) for ref in refs]
                    for refs in sources
                ]
                for d in range(3):
                    for n, target in enumerate(targets):
                        total = None
                        for i in range(EB):
                            s = i - (target - RANGE)
                            if abs(s) > RANGE:
                                continue
                            for q in range(3):
                                value = coef[(q * 3 + d) * SPAN + s + RANGE][None] * tiles[q][i]
                                total = value if total is None else total + value
                        mixed[slot, d, c * ts + j : c * ts + j + ROWS, n * ts : (n + 1) * ts] = (
                            total.reshape(ROWS, ts).astype(BF16)
                        )

    def contract(t, slot):
        for d in range(3):
            got = jnp.dot(left[t, d], mixed[slot, d], preferred_element_type=F32).astype(BF16)
            for n in range(EB):
                for c in range(2):
                    prod[slot, n * ts : (n + 1) * ts, (2 * d + c) * ts : (2 * d + c + 1) * ts] = got[
                        c * ts : (c + 1) * ts, n * ts : (n + 1) * ts
                    ]
        return jnp.dot(prod[slot], right[t], preferred_element_type=F32)

    def shift(t, way):
        return pltpu.make_async_remote_copy(
            src_ref=part.at[way, :, t], dst_ref=(from_above if way == 0 else from_below).at[:, t],
            send_sem=e_send.at[way, t], recv_sem=e_recv.at[1 - way, t],
            device_id=spot(e - 1 if way == 0 else e + 1, k), device_id_type=MESH,
        )

    early = z_hi == 0
    slow = also(low_end, early)

    def hold_near(t):
        return also(relays, t >= jnp.where(early, H0, H1))

    def hold_far(t):
        return also(relays, t >= jnp.where(early, HF0, HF1))

    ways = ((0, e > 0, z_lo == 0), (1, e < ne - 1, z_lo == ZLO - 1))

    def send_part(t, way, long, flag):
        _, there, is_long = ways[way]

        @pl.when(also(also(there, flag), is_long if long else no(is_long)))
        def _():
            shift(t, way).start()

    def send_parts(t, long, flag):
        for way in (1, 0):
            send_part(t, way, long, flag)

    def relay(t, _):
        for plane in (1, 2):
            for c in (0, 1):

                @pl.when(also(y == plane, core == c))
                def _():
                    hop = forward(t, plane, c)
                    detour(t, c, 0).wait_recv()

                    @pl.when(also(relay_waits, t == 0))
                    def _():
                        pl.semaphore_wait(ready.at[2], 1)

                    hop.start()

        return 0

    def leave(t):
        return pltpu.make_async_copy(own.at[:, t], own_out.at[:, t], own_sem.at[t])

    def keep(t, _):
        mix(t, inner, 0)
        total = contract(t, 0)
        for n in range(EB):
            for c in range(2):
                own[n, t, c] = total[n * ts : (n + 1) * ts, c * ts : (c + 1) * ts]
        leave(t).start()
        return 0

    def tile(t, _):
        for side in (0, 1):
            for i in range(EB):
                direct(t, i, side).wait_recv()
        for way in (1, 0):
            mix(t, outer[way], way)
            total = contract(t, way)
            for n in range(EB):
                for c in range(2):
                    part[way, n, t, c] = total[
                        n * ts : (n + 1) * ts, c * ts : (c + 1) * ts
                    ].astype(BF16)
            send_part(t, way, True, no(jnp.logical_or(slow, hold_far(t))))
            send_part(t, way, False, no(hold_near(t)))

        @pl.when(also(also(relays, no(early)), t < nt - ND))
        def _():
            relay(t, 0)

        @pl.when(far)
        def _():
            keep(t, 0)

        return 0

    lax.fori_loop(0, nt, tile, 0)

    def slow_parts(t, _):
        send_parts(t, True, slow)
        return 0

    @pl.when(slow)
    def _():
        pl.semaphore_wait(ready.at[3], 1)
        lax.fori_loop(0, nt, slow_parts, 0)

    @pl.when(also(relays, early))
    def _():
        lax.fori_loop(0, nt - ND, relay, 0)

    def late(t, _):
        send_parts(t, True, also(hold_far(t), no(slow)))
        send_parts(t, False, hold_near(t))
        return 0

    @pl.when(relays)
    def _():
        lax.fori_loop(0, nt, late, 0)

    @pl.when(no(far))
    def _():
        lax.fori_loop(0, nt, keep, 0)

    def finish(t, _):
        @pl.when(e > 0)
        def _():
            shift(t, 1).wait_recv()

        @pl.when(e < ne - 1)
        def _():
            shift(t, 0).wait_recv()

        return 0

    lax.fori_loop(0, nt, finish, 0)

    def drain(t, _):
        leave(t).wait()
        for way in (0, 1):
            for i in range(EB):
                direct(t, i, way).wait_send()

        @pl.when(e > 0)
        def _():
            shift(t, 0).wait_send()

        @pl.when(e < ne - 1)
        def _():
            shift(t, 1).wait_send()

        @pl.when(also(relays, t < nt - ND))
        def _():
            forward(t, 1, 0).wait_send()

        return 0

    lax.fori_loop(0, nt, drain, 0)


def solution(mesh):
    ne, nk = mesh.shape["energy"], mesh.shape["momentum"]

    def local(green_tiles, dham_blocks, phonon_weight, phonon_modes, tile_pattern):
        green = green_tiles[0]
        eb, nt, parts, ts, _ = green.shape
        dirs = dham_blocks.shape[0]
        sems = pltpu.SemaphoreType.DMA
        whole = pl.BlockSpec(memory_space=pltpu.SMEM)
        away = pl.BlockSpec(memory_space=pl.ANY)
        own, from_below, from_above = pl.pallas_call(
            functools.partial(kernel, ne, nk),
            out_shape=[jax.ShapeDtypeStruct(green.shape, kind) for kind in (F32, BF16, BF16)],
            in_specs=[whole, whole, whole, away, away],
            out_specs=[away, away, away],
            scratch_shapes=[
                pltpu.VMEM(green.shape, BF16),
                pltpu.VMEM(dham_blocks.shape, BF16),
                pltpu.VMEM((3 * dirs * SPAN, 8, 128), F32),
                pltpu.VMEM((nt, dirs, 2 * ts, 2 * ts), BF16),
                pltpu.VMEM((nt, 2 * ts * dirs, 2 * ts), BF16),
                pltpu.VMEM((2, dirs, 2 * ts, 2 * ts), BF16),
                pltpu.VMEM((2, 2 * ts, 2 * ts * dirs), BF16),
                pltpu.VMEM((2, nt, eb, parts, ts, ts), BF16),
                pltpu.VMEM((nt, parts, ts, ts), BF16),
                pltpu.VMEM((2, eb, nt, parts, ts, ts), BF16),
                pltpu.VMEM(green.shape, F32),
                pltpu.SemaphoreType.REGULAR((5,)),
                sems((3,)),
                sems((nt,)),
                sems((2, nt, eb)),
                sems((2, nt, eb)),
                sems((nt,)),
                sems((nt,)),
                sems((2, nt)),
                sems((2, nt)),
            ],
            compiler_params=pltpu.CompilerParams(collective_id=0, has_side_effects=True),
        )(phonon_weight.transpose(1, 2, 0), phonon_modes.T, tile_pattern.T, green, dham_blocks)
        return (own + from_below.astype(F32) + from_above.astype(F32)).astype(BF16)[None]

    placed = (P("momentum", "energy", None, None, None, None), P(), P(), P(), P())
    return jax.shard_map(
        local,
        mesh=mesh,
        in_specs=placed,
        out_specs=P("momentum", "energy", None, None, None, None),
        check_vma=False,
    )
```

```python
import functools

import jax
import jax.numpy as jnp
from jax import lax
from jax.experimental import pallas as pl
from jax.experimental.pallas import tpu as pltpu
from jax.sharding import PartitionSpec as P

MESH = pl.DeviceIdType.MESH
F32, BF16 = jnp.float32, jnp.bfloat16
DF, KL, NDE, ND, H0, H1, HF0, HF1 = 0, 1, 1, 1, 1, 0, 1, 1
ZLO, YS, CORES, EB, NB, RANGE = 8, 4, 2, 2, 3, 2
SPAN = 2 * RANGE + 1
ROWS = 16


def spot(e, k):
    return {"energy": e, "momentum": k}


def kernel(
    ne, nk, weight, modes, pattern, green, dham, out,
    mine, blocks, coef, left, right, mixed, prod, near, passing, part, gained, own, ready,
    load_sem, m_send, m_recv, r_send, r_recv, e_send, e_recv,
):
    nt, ts = green.shape[1], green.shape[3]
    e, k = lax.axis_index("energy"), lax.axis_index("momentum")
    core, y, z_hi = k % CORES, (k // CORES) % YS, k // (CORES * YS)
    z_lo, x = e % ZLO, e // ZLO

    def at(plane, c, side):
        turn = jnp.where(z_lo < ZLO // 2, side, 1 - side)
        return spot(
            x * ZLO + (z_lo + ZLO // 2) % ZLO, (((z_hi + turn) % 2) * YS + plane) * CORES + c
        )

    up_far = jnp.logical_and(y == YS - 1, core == 1)
    down_far = jnp.logical_and(y == 0, core == 0)
    relays = jnp.logical_or(y == 1, y == 2)
    above, below = (k + 1) % nk, (k + nk - 1) % nk

    loads = [
        pltpu.make_async_copy(green, mine, load_sem.at[0]),
        pltpu.make_async_copy(dham, blocks, load_sem.at[1]),
    ]
    for load in loads:
        load.start()

    barrier = pltpu.get_barrier_semaphore()

    def greet(where):
        pl.semaphore_signal(barrier, inc=1, device_id=where, device_id_type=MESH)

    z = z_hi * ZLO + z_lo
    edge = jnp.logical_or(z_lo % (ZLO // 2) == 0, z_lo % (ZLO // 2) == ZLO // 2 - 1)
    straight = jnp.where(edge, NDE, ND)
    passed = straight
    ahead, behind = (z + ZLO // 2) % (2 * ZLO), (z + 3 * ZLO // 2) % (2 * ZLO)

    def answered(source, target):
        return jnp.logical_and(source < ZLO, target > source)

    def relayed(source, target):
        return jnp.logical_or(target >= ZLO, answered(source, target))

    def also(flag, other):
        return jnp.logical_and(flag, other)

    def no(flag):
        return jnp.logical_not(flag)

    count, answers = jnp.int32(0), []

    def meet(flag, where):
        pl.when(flag)(lambda: greet(where))

    def expect(flag):
        nonlocal count
        count = count + flag.astype(jnp.int32)

    far_waits, relay_waits = [], jnp.bool_(False)
    for mine_far, out_plane, in_plane in ((up_far, 2, 1), (down_far, 1, 2)):
        for c, (there, back) in enumerate(((ahead, behind), (behind, ahead))):
            late = answered(z, there)
            meet(also(mine_far, late), at(out_plane, c, c))
            expect(also(mine_far, no(late)))
            if mine_far is up_far:
                far_waits.append(late)
            late = relayed(back, z)
            meet(also(mine_far, no(late)), at(in_plane, c, 1 - c))
            expect(also(mine_far, late))
            answers.append((also(mine_far, late), at(in_plane, c, 1 - c), 2))
    for mine_far, end in ((up_far, spot(e, above)), (down_far, spot(e, below))):
        if ND:
            meet(also(mine_far, z_hi == 0), end)
            expect(also(mine_far, z_hi == 1))
            answers.append((also(mine_far, z_hi == 1), end, 4))
    for plane, source, goal in ((1, (0, 0), (YS - 1, 1)), (2, (YS - 1, 1), (0, 0))):
        for c, (there, back) in enumerate(((ahead, behind), (behind, ahead))):
            here = also(y == plane, core == c)
            late = answered(back, z)
            meet(also(here, no(late)), at(*source, 1 - c))
            expect(also(here, late))
            answers.append((also(here, late), at(*source, 1 - c), c))
            late = relayed(z, there)
            meet(also(here, late), at(*goal, c))
            expect(also(here, no(late)))
            relay_waits = jnp.logical_or(relay_waits, also(here, late))

    meet(no(down_far), spot(e, below))
    meet(no(up_far), spot(e, above))
    expect(no(down_far))
    expect(no(up_far))
    low_end, high_end = also(z_lo == 0, e > 0), also(z_lo == ZLO - 1, e < ne - 1)
    meet(e > 0, spot(e - 1, k))
    meet(also(e < ne - 1, no(also(high_end, z_hi == 0))), spot(e + 1, k))
    expect(also(e > 0, no(also(low_end, z_hi == 0))))
    expect(e < ne - 1)
    answers.append((also(high_end, z_hi == 0), spot(e + 1, k), 3))
    pl.semaphore_wait(barrier, count)
    for flag, where, slot in answers:

        @pl.when(flag)
        def _():
            pl.semaphore_signal(ready.at[slot], inc=1, device_id=where, device_id_type=MESH)

    far = jnp.logical_or(up_far, down_far)

    def direct(t, i, way):
        target = above if way == 0 else below
        return pltpu.make_async_remote_copy(
            src_ref=green.at[i, t], dst_ref=near.at[way, t, i],
            send_sem=m_send.at[way, t, i], recv_sem=m_recv.at[way, t, i],
            device_id=spot(e, target), device_id_type=MESH,
        )

    def detour(t, i, way):
        return pltpu.make_async_remote_copy(
            src_ref=green.at[i, t], dst_ref=passing.at[t],
            send_sem=m_send.at[way, t, i], recv_sem=r_recv.at[t],
            device_id=at(2 if way == 0 else 1, i, i), device_id_type=MESH,
        )

    def forward(t, plane, c):
        goal_y, goal_c, way = (0, 0, 0) if plane == 2 else (YS - 1, 1, 1)
        return pltpu.make_async_remote_copy(
            src_ref=passing.at[t], dst_ref=near.at[way, t, c],
            send_sem=r_send.at[t], recv_sem=m_recv.at[way, t, c],
            device_id=at(goal_y, goal_c, c), device_id_type=MESH,
        )

    def send_near(t, _):
        for way, is_far in ((0, up_far), (1, down_far)):
            for i in range(EB):

                @pl.when(no(is_far))
                def _():
                    direct(t, i, way).start()

        return 0

    lax.fori_loop(0, nt, send_near, 0)
    for i in range(EB):

        @pl.when(also(far, far_waits[i]))
        def _():
            pl.semaphore_wait(ready.at[i], 1)

    for way, is_far in ((0, up_far), (1, down_far)):

        @pl.when(is_far)
        def _():
            def send_far(t, _):
                for i in range(EB):
                    detour(t, i, way).start()
                return 0

            def send_straight(t, _):
                for i in range(EB):
                    direct(t, i, way).start()
                return 0

            if DF:

                @pl.when(z_hi == 1)
                def _():
                    lax.fori_loop(nt - straight, nt, send_straight, 0)

            lax.fori_loop(0, nt - straight, send_far, 0)

            @pl.when(z_hi == 0)
            def _():
                pl.semaphore_wait(ready.at[4], 1)
                lax.fori_loop(nt - straight, nt, send_straight, 0)

            if not DF:

                @pl.when(z_hi == 1)
                def _():
                    lax.fori_loop(nt - straight, nt, send_straight, 0)

    for side, edge_here in ((0, e == 0), (1, e == ne - 1)):

        @pl.when(edge_here)
        def _():
            gained[side] = jnp.zeros(gained.shape[1:], BF16)

    lane = lax.broadcasted_iota(jnp.int32, (8, 128), 1)
    row = lax.broadcasted_iota(jnp.int32, (8, 128), 0)
    lane_q, lane_s = lane // SPAN - 1, lane % SPAN - RANGE
    table = jnp.zeros((8, 128), F32)
    for m in range(modes.shape[1]):
        emit, absorb = [
            jnp.where(row == 0, weight[0, i, m], jnp.where(row == 1, weight[1, i, m], weight[2, i, m]))
            for i in (0, 1)
        ]
        step = modes[1, m]
        term = jnp.where(lane_s == -step, emit, 0.0) + jnp.where(lane_s == step, absorb, 0.0)
        table = table + jnp.where(lane_q == modes[0, m], term, 0.0)
    table = table.astype(BF16).astype(F32)
    for q in range(3):
        for d in range(3):
            for s in range(SPAN):
                at_lane = q * SPAN + s
                coef[(q * 3 + d) * SPAN + s] = jnp.broadcast_to(
                    table[d : d + 1, at_lane : at_lane + 1], (8, 128)
                )

    loads[1].wait()

    def stack(t, _):
        for d in range(3):
            re, im = blocks[d, pattern[0, t], 0], blocks[d, pattern[0, t], 1]
            left[t, d, :ts, :ts] = re
            left[t, d, :ts, ts:] = -im
            left[t, d, ts:, :ts] = im
            left[t, d, ts:, ts:] = re
            re = blocks[d, pattern[1, t], 0].astype(F32).T.astype(BF16)
            im = blocks[d, pattern[1, t], 1].astype(F32).T.astype(BF16)
            base = 2 * ts * d
            right[t, base : base + ts, :ts] = re
            right[t, base : base + ts, ts:] = -im
            right[t, base + ts : base + 2 * ts, :ts] = im
            right[t, base + ts : base + 2 * ts, ts:] = re
        return 0

    lax.fori_loop(0, nt, stack, 0)

    loads[0].wait()

    outer = [[0, 1], [4, 5]]
    inner = [2, 3]

    def mix(t, targets, slot):
        sources = (
            [near.at[1, t, i] for i in range(EB)],
            [mine.at[i, t] for i in range(EB)],
            [near.at[0, t, i] for i in range(EB)],
        )
        for c in range(2):
            for j in range(0, ts, ROWS):
                tiles = [
                    [ref[c, j : j + ROWS, :].astype(F32).reshape(ROWS // 8, 8, ts) for ref in refs]
                    for refs in sources
                ]
                for d in range(3):
                    for n, target in enumerate(targets):
                        total = None
                        for i in range(EB):
                            s = i - (target - RANGE)
                            if abs(s) > RANGE:
                                continue
                            for q in range(3):
                                value = coef[(q * 3 + d) * SPAN + s + RANGE][None] * tiles[q][i]
                                total = value if total is None else total + value
                        mixed[slot, d, c * ts + j : c * ts + j + ROWS, n * ts : (n + 1) * ts] = (
                            total.reshape(ROWS, ts).astype(BF16)
                        )

    def contract(t, slot):
        for d in range(3):
            got = jnp.dot(left[t, d], mixed[slot, d], preferred_element_type=F32).astype(BF16)
            for n in range(EB):
                for c in range(2):
                    prod[slot, n * ts : (n + 1) * ts, (2 * d + c) * ts : (2 * d + c + 1) * ts] = got[
                        c * ts : (c + 1) * ts, n * ts : (n + 1) * ts
                    ]
        return jnp.dot(prod[slot], right[t], preferred_element_type=F32)

    def shift(t, way):
        return pltpu.make_async_remote_copy(
            src_ref=part.at[way, :, t], dst_ref=gained.at[1 - way, :, t],
            send_sem=e_send.at[way, t], recv_sem=e_recv.at[1 - way, t],
            device_id=spot(e - 1 if way == 0 else e + 1, k), device_id_type=MESH,
        )

    early = z_hi == 0
    slow = also(low_end, early)

    def hold_near(t):
        return also(relays, t >= jnp.where(early, H0, H1))

    def hold_far(t):
        return also(relays, t >= jnp.where(early, HF0, HF1))

    ways = ((0, e > 0, z_lo == 0), (1, e < ne - 1, z_lo == ZLO - 1))

    def send_part(t, way, long, flag):
        _, there, is_long = ways[way]

        @pl.when(also(also(there, flag), is_long if long else no(is_long)))
        def _():
            shift(t, way).start()

    def send_parts(t, long, flag):
        for way in (1, 0):
            send_part(t, way, long, flag)

    def relay(t, _):
        for plane in (1, 2):
            for c in (0, 1):

                @pl.when(also(y == plane, core == c))
                def _():
                    hop = forward(t, plane, c)
                    detour(t, c, 0).wait_recv()

                    @pl.when(also(relay_waits, t == 0))
                    def _():
                        pl.semaphore_wait(ready.at[2], 1)

                    hop.start()

        return 0

    def keep(t, _):
        mix(t, inner, 0)
        total = contract(t, 0)
        for n in range(EB):
            for c in range(2):
                own[n, t, c] = total[n * ts : (n + 1) * ts, c * ts : (c + 1) * ts]
        return 0

    def tile(t, _):
        for side in (0, 1):
            for i in range(EB):
                direct(t, i, side).wait_recv()
        for way in (1, 0):
            mix(t, outer[way], way)
            total = contract(t, way)
            for n in range(EB):
                for c in range(2):
                    part[way, n, t, c] = total[
                        n * ts : (n + 1) * ts, c * ts : (c + 1) * ts
                    ].astype(BF16)
            send_part(t, way, True, no(jnp.logical_or(slow, hold_far(t))))
            send_part(t, way, False, no(hold_near(t)))

        @pl.when(also(also(relays, no(early)), t < nt - passed))
        def _():
            relay(t, 0)

        if not KL:

            @pl.when(far)
            def _():
                keep(t, 0)

        return 0

    lax.fori_loop(0, nt, tile, 0)

    def slow_parts(t, _):
        send_parts(t, True, slow)
        return 0

    @pl.when(slow)
    def _():
        pl.semaphore_wait(ready.at[3], 1)
        lax.fori_loop(0, nt, slow_parts, 0)

    @pl.when(also(relays, early))
    def _():
        lax.fori_loop(0, nt - passed, relay, 0)

    def late(t, _):
        send_parts(t, True, also(hold_far(t), no(slow)))
        send_parts(t, False, hold_near(t))
        return 0

    @pl.when(relays)
    def _():
        lax.fori_loop(0, nt, late, 0)

    if KL:
        lax.fori_loop(0, nt, keep, 0)
    else:

        @pl.when(no(far))
        def _():
            lax.fori_loop(0, nt, keep, 0)

    def finish(t, _):
        @pl.when(e > 0)
        def _():
            shift(t, 1).wait_recv()

        @pl.when(e < ne - 1)
        def _():
            shift(t, 0).wait_recv()

        for n in range(EB):
            out[n, t] = (
                own[n, t] + gained[0, n, t].astype(F32) + gained[1, n, t].astype(F32)
            ).astype(BF16)
        return 0

    lax.fori_loop(0, nt, finish, 0)

    def drain(t, _):
        for way in (0, 1):
            for i in range(EB):
                direct(t, i, way).wait_send()

        @pl.when(e > 0)
        def _():
            shift(t, 0).wait_send()

        @pl.when(e < ne - 1)
        def _():
            shift(t, 1).wait_send()

        @pl.when(also(relays, t < nt - passed))
        def _():
            forward(t, 1, 0).wait_send()

        return 0

    lax.fori_loop(0, nt, drain, 0)


def solution(mesh):
    ne, nk = mesh.shape["energy"], mesh.shape["momentum"]

    def local(green_tiles, dham_blocks, phonon_weight, phonon_modes, tile_pattern):
        green = green_tiles[0]
        eb, nt, parts, ts, _ = green.shape
        dirs = dham_blocks.shape[0]
        sems = pltpu.SemaphoreType.DMA
        whole = pl.BlockSpec(memory_space=pltpu.SMEM)
        away = pl.BlockSpec(memory_space=pl.ANY)
        summed = pl.pallas_call(
            functools.partial(kernel, ne, nk),
            out_shape=pltpu.VMEM(green.shape, BF16),
            in_specs=[whole, whole, whole, away, away],
            out_specs=pl.BlockSpec(memory_space=pltpu.VMEM),
            scratch_shapes=[
                pltpu.VMEM(green.shape, BF16),
                pltpu.VMEM(dham_blocks.shape, BF16),
                pltpu.VMEM((3 * dirs * SPAN, 8, 128), F32),
                pltpu.VMEM((nt, dirs, 2 * ts, 2 * ts), BF16),
                pltpu.VMEM((nt, 2 * ts * dirs, 2 * ts), BF16),
                pltpu.VMEM((2, dirs, 2 * ts, 2 * ts), BF16),
                pltpu.VMEM((2, 2 * ts, 2 * ts * dirs), BF16),
                pltpu.VMEM((2, nt, eb, parts, ts, ts), BF16),
                pltpu.VMEM((nt, parts, ts, ts), BF16),
                pltpu.VMEM((2, eb, nt, parts, ts, ts), BF16),
                pltpu.VMEM((2, *green.shape), BF16),
                pltpu.VMEM(green.shape, F32),
                pltpu.SemaphoreType.REGULAR((5,)),
                sems((2,)),
                sems((2, nt, eb)),
                sems((2, nt, eb)),
                sems((nt,)),
                sems((nt,)),
                sems((2, nt)),
                sems((2, nt)),
            ],
            compiler_params=pltpu.CompilerParams(collective_id=0, has_side_effects=True),
        )(phonon_weight.transpose(1, 2, 0), phonon_modes.T, tile_pattern.T, green, dham_blocks)
        return summed[None]

    placed = (P("momentum", "energy", None, None, None, None), P(), P(), P(), P())
    return jax.shard_map(
        local,
        mesh=mesh,
        in_specs=placed,
        out_specs=P("momentum", "energy", None, None, None, None),
        check_vma=False,
    )
```

```python
import functools

import jax
import jax.numpy as jnp
from jax import lax
from jax.experimental import pallas as pl
from jax.experimental.pallas import tpu as pltpu
from jax.sharding import PartitionSpec as P

MESH = pl.DeviceIdType.MESH
F32, BF16 = jnp.float32, jnp.bfloat16
DF, KL, NDE, ND, H0, H1, HF0, HF1 = 0, 1, 1, 1, 1, 0, 1, 1
ZLO, YS, CORES, EB, NB, RANGE = 8, 4, 2, 2, 3, 2
SPAN = 2 * RANGE + 1
ROWS = 16


def spot(e, k):
    return {"energy": e, "momentum": k}


def kernel(
    ne, nk, weight, modes, pattern, green, dham, out,
    mine, blocks, coef, left, right, mixed, prod, near, passing, part, gained, own, ready,
    load_sem, m_send, m_recv, r_send, r_recv, e_send, e_recv,
):
    nt, ts = green.shape[1], green.shape[3]
    e, k = lax.axis_index("energy"), lax.axis_index("momentum")
    core, y, z_hi = k % CORES, (k // CORES) % YS, k // (CORES * YS)
    z_lo, x = e % ZLO, e // ZLO

    def at(plane, c, side):
        turn = jnp.where(z_lo < ZLO // 2, side, 1 - side)
        return spot(
            x * ZLO + (z_lo + ZLO // 2) % ZLO, (((z_hi + turn) % 2) * YS + plane) * CORES + c
        )

    up_far = jnp.logical_and(y == YS - 1, core == 1)
    down_far = jnp.logical_and(y == 0, core == 0)
    relays = jnp.logical_or(y == 1, y == 2)
    above, below = (k + 1) % nk, (k + nk - 1) % nk

    loads = [
        pltpu.make_async_copy(green, mine, load_sem.at[0]),
        pltpu.make_async_copy(dham, blocks, load_sem.at[1]),
    ]
    for load in loads:
        load.start()

    barrier = pltpu.get_barrier_semaphore()

    def greet(where):
        pl.semaphore_signal(barrier, inc=1, device_id=where, device_id_type=MESH)

    z = z_hi * ZLO + z_lo
    edge = jnp.logical_or(z_lo % (ZLO // 2) == 0, z_lo % (ZLO // 2) == ZLO // 2 - 1)
    straight = jnp.where(edge, NDE, ND)
    passed = straight
    ahead, behind = (z + ZLO // 2) % (2 * ZLO), (z + 3 * ZLO // 2) % (2 * ZLO)

    def answered(source, target):
        return jnp.logical_and(source < ZLO, target > source)

    def relayed(source, target):
        return jnp.logical_or(target >= ZLO, answered(source, target))

    def also(flag, other):
        return jnp.logical_and(flag, other)

    def no(flag):
        return jnp.logical_not(flag)

    count, answers = jnp.int32(0), []

    def meet(flag, where):
        pl.when(flag)(lambda: greet(where))

    def expect(flag):
        nonlocal count
        count = count + flag.astype(jnp.int32)

    far_waits, relay_waits = [], jnp.bool_(False)
    for mine_far, out_plane, in_plane in ((up_far, 2, 1), (down_far, 1, 2)):
        for c, (there, back) in enumerate(((ahead, behind), (behind, ahead))):
            late = answered(z, there)
            meet(also(mine_far, late), at(out_plane, c, c))
            expect(also(mine_far, no(late)))
            if mine_far is up_far:
                far_waits.append(late)
            late = relayed(back, z)
            meet(also(mine_far, no(late)), at(in_plane, c, 1 - c))
            expect(also(mine_far, late))
            answers.append((also(mine_far, late), at(in_plane, c, 1 - c), 2))
    for mine_far, end in ((up_far, spot(e, above)), (down_far, spot(e, below))):
        if ND:
            meet(also(mine_far, z_hi == 0), end)
            expect(also(mine_far, z_hi == 1))
            answers.append((also(mine_far, z_hi == 1), end, 4))
    for plane, source, goal in ((1, (0, 0), (YS - 1, 1)), (2, (YS - 1, 1), (0, 0))):
        for c, (there, back) in enumerate(((ahead, behind), (behind, ahead))):
            here = also(y == plane, core == c)
            late = answered(back, z)
            meet(also(here, no(late)), at(*source, 1 - c))
            expect(also(here, late))
            answers.append((also(here, late), at(*source, 1 - c), c))
            late = relayed(z, there)
            meet(also(here, late), at(*goal, c))
            expect(also(here, no(late)))
            relay_waits = jnp.logical_or(relay_waits, also(here, late))

    meet(no(down_far), spot(e, below))
    meet(no(up_far), spot(e, above))
    expect(no(down_far))
    expect(no(up_far))
    low_end, high_end = also(z_lo == 0, e > 0), also(z_lo == ZLO - 1, e < ne - 1)
    meet(e > 0, spot(e - 1, k))
    meet(also(e < ne - 1, no(also(high_end, z_hi == 0))), spot(e + 1, k))
    expect(also(e > 0, no(also(low_end, z_hi == 0))))
    expect(e < ne - 1)
    answers.append((also(high_end, z_hi == 0), spot(e + 1, k), 3))
    pl.semaphore_wait(barrier, count)
    for flag, where, slot in answers:

        @pl.when(flag)
        def _():
            pl.semaphore_signal(ready.at[slot], inc=1, device_id=where, device_id_type=MESH)

    far = jnp.logical_or(up_far, down_far)

    def direct(t, i, way):
        target = above if way == 0 else below
        return pltpu.make_async_remote_copy(
            src_ref=green.at[i, t], dst_ref=near.at[way, t, i],
            send_sem=m_send.at[way, t, i], recv_sem=m_recv.at[way, t, i],
            device_id=spot(e, target), device_id_type=MESH,
        )

    def detour(t, i, way):
        return pltpu.make_async_remote_copy(
            src_ref=green.at[i, t], dst_ref=passing.at[t],
            send_sem=m_send.at[way, t, i], recv_sem=r_recv.at[t],
            device_id=at(2 if way == 0 else 1, i, i), device_id_type=MESH,
        )

    def forward(t, plane, c):
        goal_y, goal_c, way = (0, 0, 0) if plane == 2 else (YS - 1, 1, 1)
        return pltpu.make_async_remote_copy(
            src_ref=passing.at[t], dst_ref=near.at[way, t, c],
            send_sem=r_send.at[t], recv_sem=m_recv.at[way, t, c],
            device_id=at(goal_y, goal_c, c), device_id_type=MESH,
        )

    def send_near(t, _):
        for way, is_far in ((0, up_far), (1, down_far)):
            for i in range(EB):

                @pl.when(no(is_far))
                def _():
                    direct(t, i, way).start()

        return 0

    @pl.when(no(also(far, z_hi == 1)))
    def _():
        lax.fori_loop(0, nt, send_near, 0)

    for i in range(EB):

        @pl.when(also(far, far_waits[i]))
        def _():
            pl.semaphore_wait(ready.at[i], 1)

    for way, is_far in ((0, up_far), (1, down_far)):

        @pl.when(is_far)
        def _():
            def send_far(t, _):
                for i in range(EB):
                    detour(t, i, way).start()
                return 0

            def send_straight(t, _):
                for i in range(EB):
                    direct(t, i, way).start()
                return 0

            if DF:

                @pl.when(z_hi == 1)
                def _():
                    lax.fori_loop(nt - straight, nt, send_straight, 0)

            lax.fori_loop(0, nt - straight, send_far, 0)

            @pl.when(z_hi == 0)
            def _():
                pl.semaphore_wait(ready.at[4], 1)
                lax.fori_loop(nt - straight, nt, send_straight, 0)

            if not DF:

                @pl.when(z_hi == 1)
                def _():
                    lax.fori_loop(nt - straight, nt, send_straight, 0)

    @pl.when(also(far, z_hi == 1))
    def _():
        lax.fori_loop(0, nt, send_near, 0)

    for side, edge_here in ((0, e == 0), (1, e == ne - 1)):

        @pl.when(edge_here)
        def _():
            gained[side] = jnp.zeros(gained.shape[1:], BF16)

    lane = lax.broadcasted_iota(jnp.int32, (8, 128), 1)
    row = lax.broadcasted_iota(jnp.int32, (8, 128), 0)
    lane_q, lane_s = lane // SPAN - 1, lane % SPAN - RANGE
    table = jnp.zeros((8, 128), F32)
    for m in range(modes.shape[1]):
        emit, absorb = [
            jnp.where(row == 0, weight[0, i, m], jnp.where(row == 1, weight[1, i, m], weight[2, i, m]))
            for i in (0, 1)
        ]
        step = modes[1, m]
        term = jnp.where(lane_s == -step, emit, 0.0) + jnp.where(lane_s == step, absorb, 0.0)
        table = table + jnp.where(lane_q == modes[0, m], term, 0.0)
    table = table.astype(BF16).astype(F32)
    for q in range(3):
        for d in range(3):
            for s in range(SPAN):
                at_lane = q * SPAN + s
                coef[(q * 3 + d) * SPAN + s] = jnp.broadcast_to(
                    table[d : d + 1, at_lane : at_lane + 1], (8, 128)
                )

    loads[1].wait()

    def stack(t, _):
        for d in range(3):
            re, im = blocks[d, pattern[0, t], 0], blocks[d, pattern[0, t], 1]
            left[t, d, :ts, :ts] = re
            left[t, d, :ts, ts:] = -im
            left[t, d, ts:, :ts] = im
            left[t, d, ts:, ts:] = re
            re = blocks[d, pattern[1, t], 0].astype(F32).T.astype(BF16)
            im = blocks[d, pattern[1, t], 1].astype(F32).T.astype(BF16)
            base = 2 * ts * d
            right[t, base : base + ts, :ts] = re
            right[t, base : base + ts, ts:] = -im
            right[t, base + ts : base + 2 * ts, :ts] = im
            right[t, base + ts : base + 2 * ts, ts:] = re
        return 0

    lax.fori_loop(0, nt, stack, 0)

    loads[0].wait()

    outer = [[0, 1], [4, 5]]
    inner = [2, 3]

    def mix(t, targets, slot):
        sources = (
            [near.at[1, t, i] for i in range(EB)],
            [mine.at[i, t] for i in range(EB)],
            [near.at[0, t, i] for i in range(EB)],
        )
        for c in range(2):
            for j in range(0, ts, ROWS):
                tiles = [
                    [ref[c, j : j + ROWS, :].astype(F32).reshape(ROWS // 8, 8, ts) for ref in refs]
                    for refs in sources
                ]
                for d in range(3):
                    for n, target in enumerate(targets):
                        total = None
                        for i in range(EB):
                            s = i - (target - RANGE)
                            if abs(s) > RANGE:
                                continue
                            for q in range(3):
                                value = coef[(q * 3 + d) * SPAN + s + RANGE][None] * tiles[q][i]
                                total = value if total is None else total + value
                        mixed[slot, d, c * ts + j : c * ts + j + ROWS, n * ts : (n + 1) * ts] = (
                            total.reshape(ROWS, ts).astype(BF16)
                        )

    def contract(t, slot):
        for d in range(3):
            got = jnp.dot(left[t, d], mixed[slot, d], preferred_element_type=F32).astype(BF16)
            for n in range(EB):
                for c in range(2):
                    prod[slot, n * ts : (n + 1) * ts, (2 * d + c) * ts : (2 * d + c + 1) * ts] = got[
                        c * ts : (c + 1) * ts, n * ts : (n + 1) * ts
                    ]
        return jnp.dot(prod[slot], right[t], preferred_element_type=F32)

    def shift(t, way):
        return pltpu.make_async_remote_copy(
            src_ref=part.at[way, :, t], dst_ref=gained.at[1 - way, :, t],
            send_sem=e_send.at[way, t], recv_sem=e_recv.at[1 - way, t],
            device_id=spot(e - 1 if way == 0 else e + 1, k), device_id_type=MESH,
        )

    early = z_hi == 0
    slow = also(low_end, early)

    def hold_near(t):
        return also(relays, t >= jnp.where(early, H0, H1))

    def hold_far(t):
        return also(relays, t >= jnp.where(early, HF0, HF1))

    ways = ((0, e > 0, z_lo == 0), (1, e < ne - 1, z_lo == ZLO - 1))

    def send_part(t, way, long, flag):
        _, there, is_long = ways[way]

        @pl.when(also(also(there, flag), is_long if long else no(is_long)))
        def _():
            shift(t, way).start()

    def send_parts(t, long, flag):
        for way in (1, 0):
            send_part(t, way, long, flag)

    def relay(t, _):
        for plane in (1, 2):
            for c in (0, 1):

                @pl.when(also(y == plane, core == c))
                def _():
                    hop = forward(t, plane, c)
                    detour(t, c, 0).wait_recv()

                    @pl.when(also(relay_waits, t == 0))
                    def _():
                        pl.semaphore_wait(ready.at[2], 1)

                    hop.start()

        return 0

    def keep(t, _):
        mix(t, inner, 0)
        total = contract(t, 0)
        for n in range(EB):
            for c in range(2):
                own[n, t, c] = total[n * ts : (n + 1) * ts, c * ts : (c + 1) * ts]
        return 0

    def tile(t, _):
        for side in (0, 1):
            for i in range(EB):
                direct(t, i, side).wait_recv()
        for way in (1, 0):
            mix(t, outer[way], way)
            total = contract(t, way)
            for n in range(EB):
                for c in range(2):
                    part[way, n, t, c] = total[
                        n * ts : (n + 1) * ts, c * ts : (c + 1) * ts
                    ].astype(BF16)
            send_part(t, way, True, no(jnp.logical_or(slow, hold_far(t))))
            send_part(t, way, False, no(hold_near(t)))

        @pl.when(also(also(relays, no(early)), t < nt - passed))
        def _():
            relay(t, 0)

        if not KL:

            @pl.when(far)
            def _():
                keep(t, 0)

        return 0

    lax.fori_loop(0, nt, tile, 0)

    def slow_parts(t, _):
        send_parts(t, True, slow)
        return 0

    @pl.when(slow)
    def _():
        pl.semaphore_wait(ready.at[3], 1)
        lax.fori_loop(0, nt, slow_parts, 0)

    @pl.when(also(relays, early))
    def _():
        lax.fori_loop(0, nt - passed, relay, 0)

    def late(t, _):
        send_parts(t, True, also(hold_far(t), no(slow)))
        send_parts(t, False, hold_near(t))
        return 0

    @pl.when(relays)
    def _():
        lax.fori_loop(0, nt, late, 0)

    if KL:
        lax.fori_loop(0, nt, keep, 0)
    else:

        @pl.when(no(far))
        def _():
            lax.fori_loop(0, nt, keep, 0)

    def finish(t, _):
        @pl.when(e > 0)
        def _():
            shift(t, 1).wait_recv()

        @pl.when(e < ne - 1)
        def _():
            shift(t, 0).wait_recv()

        for n in range(EB):
            out[n, t] = (
                own[n, t] + gained[0, n, t].astype(F32) + gained[1, n, t].astype(F32)
            ).astype(BF16)
        return 0

    lax.fori_loop(0, nt, finish, 0)

    def drain(t, _):
        for way in (0, 1):
            for i in range(EB):
                direct(t, i, way).wait_send()

        @pl.when(e > 0)
        def _():
            shift(t, 0).wait_send()

        @pl.when(e < ne - 1)
        def _():
            shift(t, 1).wait_send()

        @pl.when(also(relays, t < nt - passed))
        def _():
            forward(t, 1, 0).wait_send()

        return 0

    lax.fori_loop(0, nt, drain, 0)


def solution(mesh):
    ne, nk = mesh.shape["energy"], mesh.shape["momentum"]

    def local(green_tiles, dham_blocks, phonon_weight, phonon_modes, tile_pattern):
        green = green_tiles[0]
        eb, nt, parts, ts, _ = green.shape
        dirs = dham_blocks.shape[0]
        sems = pltpu.SemaphoreType.DMA
        whole = pl.BlockSpec(memory_space=pltpu.SMEM)
        away = pl.BlockSpec(memory_space=pl.ANY)
        summed = pl.pallas_call(
            functools.partial(kernel, ne, nk),
            out_shape=pltpu.VMEM(green.shape, BF16),
            in_specs=[whole, whole, whole, away, away],
            out_specs=pl.BlockSpec(memory_space=pltpu.VMEM),
            scratch_shapes=[
                pltpu.VMEM(green.shape, BF16),
                pltpu.VMEM(dham_blocks.shape, BF16),
                pltpu.VMEM((3 * dirs * SPAN, 8, 128), F32),
                pltpu.VMEM((nt, dirs, 2 * ts, 2 * ts), BF16),
                pltpu.VMEM((nt, 2 * ts * dirs, 2 * ts), BF16),
                pltpu.VMEM((2, dirs, 2 * ts, 2 * ts), BF16),
                pltpu.VMEM((2, 2 * ts, 2 * ts * dirs), BF16),
                pltpu.VMEM((2, nt, eb, parts, ts, ts), BF16),
                pltpu.VMEM((nt, parts, ts, ts), BF16),
                pltpu.VMEM((2, eb, nt, parts, ts, ts), BF16),
                pltpu.VMEM((2, *green.shape), BF16),
                pltpu.VMEM(green.shape, F32),
                pltpu.SemaphoreType.REGULAR((5,)),
                sems((2,)),
                sems((2, nt, eb)),
                sems((2, nt, eb)),
                sems((nt,)),
                sems((nt,)),
                sems((2, nt)),
                sems((2, nt)),
            ],
            compiler_params=pltpu.CompilerParams(collective_id=0, has_side_effects=True),
        )(phonon_weight.transpose(1, 2, 0), phonon_modes.T, tile_pattern.T, green, dham_blocks)
        return summed[None]

    placed = (P("momentum", "energy", None, None, None, None), P(), P(), P(), P())
    return jax.shard_map(
        local,
        mesh=mesh,
        in_specs=placed,
        out_specs=P("momentum", "energy", None, None, None, None),
        check_vma=False,
    )
```
